32 devices in a mesh: groups: 2 (over y), rows: 8 (over z, x), layers: 2 (over core).
Axes of the slice: x: 2, y: 2, z: 4, core: 2. Of those that a mesh axis runs over, the one named last changes fastest.
Arguments:
- train_grads: bfloat16 [6144, 2, 4096], P(('groups', 'rows'), 'layers'), parts along dimension 0, may hold values from -6 to 6
- query_grads: bfloat16 [2, 2048, 4096], P('layers', ('groups', 'rows')), parts along dimension 1, may hold values from -0.09375 to 0.09375
Outputs:
- scores: float32 [1024, 6144], P('layers', ('groups', 'rows')), parts along dimension 1
The draws below stay inside these ranges and needn't reach their ends.
There are 2 independent parts, one for each index of `groups`. The reference program is written for one: setup_inputs(seed, part) draws one part's arguments, and reference() takes and returns one part's arrays. A program takes and returns all parts, laid end to end along the dimension named above; each array names one. Nothing has to cross between parts.
All inputs are finite; a program needn't handle non-finite values.
Results may differ from the reference program's by a relative error of at most 0.0003.
Values may be sent and summed in bfloat16 or wider, within the bound.
No kernel may reach another device: no remote copies, remote signals or barrier semaphores. Data moves between devices by JAX's collectives and lax.ppermute only.
A program may use at most 64 MiB of HBM per device.

```python
import jax
import jax.numpy as jnp
from jax import lax

K = 4096
Q = 1024
L = 2
NTRAIN = 3072


def spiked(array, own_key, source, target, blocks, factor):
    owner, partner = [(jnp.arange(array.shape[dim]) // (array.shape[dim] // blocks)).reshape([-1 if axis == dim else 1 for axis in range(array.ndim)]) for dim in (source, target)]
    chosen = jax.random.permutation(own_key, blocks)[partner]
    strong = (owner == chosen) | (owner == (partner + blocks // 2) % blocks)
    return jnp.where(strong, factor * array, array)


def levels(key, shape, pieces, low, high):
    level = 1.0
    for dim, parts in pieces:
        steps = jax.random.uniform(jax.random.fold_in(jax.random.fold_in(key, 6), dim), (parts,), jnp.float32, low / len(pieces), high / len(pieces))
        level = level * jnp.repeat(jnp.exp(steps), shape[dim] // parts).reshape((-1,) + (1,) * (len(shape) - 1 - dim))
    return level


def normal_values(stream_key, shape, deviation, bound, cuts=(), kind=jnp.bfloat16):
    factor_of = levels(stream_key, shape, cuts, -0.22, 0.18) if cuts else 1.0
    array = jax.random.normal(stream_key, shape, jnp.float32) * deviation * factor_of
    return jnp.minimum(jnp.maximum(array, -bound), bound).astype(kind)


def bell_draw_with(own_key, extent, spread, most, pieces, heavy, held_as=jnp.bfloat16):
    result = spread * jax.random.normal(own_key, extent, jnp.float32)
    if pieces:
        result = result * levels(own_key, extent, pieces, -0.22, 0.18)
    return jnp.clip(spiked(result, jax.random.fold_in(own_key, 3), *heavy), -most, most).astype(held_as)


def setup_inputs(seed: int = 0, part: int = 0) -> dict:
    streams_of = jax.random.split(jax.random.key(seed), 3)
    own_keys = jax.random.split(jax.random.fold_in(streams_of[2], part), 3)
    return {
        "train_grads": normal_values(own_keys[0], (NTRAIN, L, K), 1.0, 6.0, ((0, 8), (1, 2))),
        "query_grads": bell_draw_with(own_keys[1], (L, Q, K), (K * L) ** -0.5, 0.09375, ((0, 2), (1, 8)), (0, 1, 2, 2.0)),
    }


def reference(train_grads, query_grads):
    def layer_step(total, index):
        block = lax.dynamic_index_in_dim(train_grads, index, 1, keepdims=False)
        queries = lax.dynamic_index_in_dim(query_grads, index, 0, keepdims=False)
        part = lax.dot_general(queries, block, (((1,), (1,)), ((), ())), preferred_element_type=jnp.float32)
        return total + part, None

    start = jnp.zeros((query_grads.shape[1], train_grads.shape[0]), jnp.float32)
    total, unused = lax.scan(layer_step, start, jnp.arange(train_grads.shape[1], dtype=jnp.int32))
    return total
```

```python
import functools

import jax
import jax.numpy as jnp
import numpy as np
from jax import lax
from jax.experimental import pallas as pl
from jax.experimental.pallas import tpu as pltpu
from jax.sharding import PartitionSpec as P


NT = (((1,), (1,)), ((), ()))


def product(left, right):
    return lax.dot_general(left, right, NT, preferred_element_type=jnp.float32)


def place_rows(count, blocks, me_ref, table_ref, *refs):
    out_ref = refs[-1]
    rows = refs[0].shape[0]
    first = me_ref[1] * blocks
    for slot in range(count):
        block = table_ref[me_ref[0], slot] - first

        @pl.when((block >= 0) & (block < blocks))
        def _(slot=slot, block=block):
            at = pl.multiple_of(block * rows, rows)
            out_ref[pl.ds(at, rows), :] = refs[2 * slot][...] + refs[2 * slot + 1][...]


def shards(train_grads, query_grads):
    rows, layers = lax.axis_size("rows"), lax.axis_size("layers")
    train = train_grads.reshape(train_grads.shape[0], -1)
    queries = jnp.swapaxes(query_grads, 0, 1).reshape(query_grads.shape[1], -1)
    size, depth = queries.shape
    count = rows // 2

    ring = [2 * z for z in range(count)] + [2 * z + 1 for z in reversed(range(count))]
    ahead = [(ring[i], ring[(i + 1) % rows]) for i in range(rows)]
    back = [(target, source) for source, target in ahead]
    place = {row: i for i, row in enumerate(ring)}

    half = depth // 2
    right, left = [queries[:, :half], queries[:, half:]], [queries[:, :half], queries[:, half:]]

    def scores(pieces):
        return product(pieces[0], train[:, :half]) + product(pieces[1], train[:, half:])

    def move(piece, pairs):
        return lax.ppermute(piece, "rows", pairs)

    sums, offsets = [product(queries, train)], [0]
    for step in range(1, count + 1):
        if step < count:
            right = [move(piece, ahead) for piece in right]
            left = [move(piece, back) for piece in left]
            sums += [scores(right), scores(left)]
            offsets += [-step, step]
        else:
            last = [move(right[0], ahead), move(left[1], back)]
            sums.append(scores(last))
            offsets.append(step)

    table = np.array([[ring[(place[row] + by) % rows] for by in offsets] for row in range(rows)], np.int32)
    me = jnp.stack([lax.axis_index("rows"), lax.axis_index("layers")]).astype(jnp.int32)
    if layers != 2:
        total = jnp.zeros((rows * size, train.shape[0]), jnp.float32)
        for slot, value in enumerate(sums):
            total = lax.dynamic_update_slice_in_dim(total, value, jnp.asarray(table)[me[0], slot] * size, 0)
        return lax.psum_scatter(total, "layers", scatter_dimension=0, tiled=True)
    operands = []
    for value in sums:
        operands += [value, lax.ppermute(value, "layers", [(0, 1), (1, 0)])]
    return pl.pallas_call(
        functools.partial(place_rows, len(sums), rows // layers),
        out_shape=jax.ShapeDtypeStruct((rows * size // layers, train.shape[0]), jnp.float32),
        in_specs=[pl.BlockSpec(memory_space=pltpu.SMEM)] * 2 + [pl.BlockSpec(memory_space=pltpu.VMEM)] * len(operands),
        out_specs=pl.BlockSpec(memory_space=pltpu.VMEM),
    )(me, table, *operands)


def solution(mesh):
    in_specs = (P(("groups", "rows"), "layers", None), P("layers", ("groups", "rows"), None))
    out_specs = P("layers", ("groups", "rows"))
    return jax.shard_map(shards, mesh=mesh, in_specs=in_specs, out_specs=out_specs, check_vma=False)
```

```python
import functools

import jax
import jax.numpy as jnp
from jax import lax
from jax.experimental import pallas as pl
from jax.experimental.pallas import tpu as pltpu
from jax.sharding import PartitionSpec as P


NT = (((1,), (1,)), ((), ()))


def product(left, right):
    return lax.dot_general(left, right, NT, preferred_element_type=jnp.float32)


def gathered(train_grads, query_grads):
    terms = jnp.einsum(
        "lqk,nlk->qn",
        lax.all_gather(query_grads, "rows", axis=1, tiled=True),
        train_grads,
        preferred_element_type=jnp.float32,
    )
    return lax.psum_scatter(terms, "layers", scatter_dimension=0, tiled=True)


def place(sizes, half, group, plan, row_ref, *refs):
    out_ref, both_ref, sem = refs[-3:]
    row = row_ref[0]
    z, x = row // 2, row % 2
    for across, low, rows, terms in plan:
        value = None
        for array, first in terms:
            term = refs[array][first : first + rows, :]
            value = term if value is None else value + term
        at = pl.multiple_of((1 - x if across else x) * sizes + low, rows)
        both_ref[pl.ds(at, rows), :] = value
    at = pl.multiple_of(lax.rem(z - group + half, half) * 2 * sizes, 2 * sizes)
    copy = pltpu.make_async_copy(both_ref, out_ref.at[pl.ds(at, 2 * sizes), :], sem)
    copy.start()
    copy.wait()


def paired(train_grads, query_grads):
    rows, layers = lax.axis_size("rows"), lax.axis_size("layers")
    count = rows // 2
    half = count // layers
    train = train_grads.reshape(train_grads.shape[0], -1)
    queries = jnp.swapaxes(query_grads, 0, 1).reshape(query_grads.shape[1], -1)
    size, depth = queries.shape
    row, core = lax.axis_index("rows"), lax.axis_index("layers")
    z, x = row // 2, row % 2
    ring = [(2 * a + b, 2 * ((a + 1) % count) + b) for a in range(count) for b in range(2)]
    swap = [(a, a ^ 1) for a in range(rows)]

    def move(value, hops):
        return lax.ppermute(value, "rows", hops)

    def cores(value):
        return lax.ppermute(value, "layers", [(0, 1), (1, 0)])

    def columns(value, which):
        return lax.dynamic_slice_in_dim(value, which * (depth // 2), depth // 2, 1)

    cut = size // 2
    low, high = queries[:, : depth // 2], queries[:, depth // 2 :]
    held = jnp.where(x == 0, low, high)
    given = [jnp.where(x == 0, high[rows], low[rows]) for rows in (slice(0, cut), slice(cut, size))]
    firsts = {"A": held, "B": move(given[0], swap), "C": move(given[1], swap)}
    sides = {"O": columns(train, x), "N": move(columns(train, 1 - x), swap)}
    partial = {}
    for piece, value in firsts.items():
        for step in range(count):
            if step:
                value = move(value, ring)
            for side, rhs in sides.items():
                partial[side, piece, step] = product(value, rhs)

    total = None
    for group in range(half):
        mine = lax.rem(z - group + count, count) // half == core
        sums, crossed = {}, {}
        for pieces in ("A", "BC"):
            for side in "NO":
                values = [partial[side, piece, step] for step in (group, group + half) for piece in pieces]
                values = lax.optimization_barrier(values)
                one, two = [jnp.concatenate(part) for part in (values[: len(pieces)], values[len(pieces) :])]
                keep, give = jnp.where(mine, one, two), jnp.where(mine, two, one)
                sums[side] = [keep, cores(give)]
            got = move(sum(sums["N"]), swap)
            first = 0
            for piece in pieces:
                height = size if piece == "A" else cut
                for at in range(first, first + height, cut):
                    key = (piece, at - first if piece == "A" else 0)
                    crossed[key] = (got, at)
                    sums[key] = [(value, at) for value in sums["O"]]
                first += height
        plan = []
        operands = []

        def index_of(value):
            for i, other in enumerate(operands):
                if other is value:
                    return i
            operands.append(value)
            return len(operands) - 1

        for mine_key, their_key, across, at in (
            (("A", 0), ("B", 0), False, 0),
            (("A", cut), ("C", 0), False, cut),
            (("B", 0), ("A", 0), True, 0),
            (("C", 0), ("A", cut), True, cut),
        ):
            terms = [*sums[mine_key], crossed[their_key]]
            plan.append((across, at, cut, [(index_of(value), first) for value, first in terms]))
        specs = [pl.BlockSpec(memory_space=pltpu.SMEM)] + [pl.BlockSpec(memory_space=pltpu.VMEM)] * len(operands)
        aliases = {}
        if total is not None:
            aliases = {len(operands) + 1: 0}
            operands.append(total)
            specs.append(pl.BlockSpec(memory_space=pl.ANY))
        total = pl.pallas_call(
            functools.partial(place, size, half, group, plan),
            out_shape=jax.ShapeDtypeStruct((rows * size // layers, train.shape[0]), jnp.float32),
            in_specs=specs,
            out_specs=pl.BlockSpec(memory_space=pl.ANY),
            scratch_shapes=[pltpu.VMEM((2 * size, train.shape[0]), jnp.float32), pltpu.SemaphoreType.DMA],
            input_output_aliases=aliases,
            compiler_params=pltpu.CompilerParams(vmem_limit_bytes=8 * 2**20),
        )(row.astype(jnp.int32).reshape(1), *operands)
    return total


def solution(mesh):
    in_specs = (P(("groups", "rows"), "layers", None), P("layers", ("groups", "rows"), None))
    out_specs = P("layers", ("groups", "rows"))
    special = mesh.shape["rows"] == 8 and mesh.shape["layers"] == 2
    shards = paired if special else gathered
    return jax.shard_map(shards, mesh=mesh, in_specs=in_specs, out_specs=out_specs, check_vma=False)
```

```python
import functools
import math

import jax
import jax.numpy as jnp
from jax import lax
from jax.experimental import pallas as pl
from jax.experimental.pallas import tpu as pltpu
from jax.sharding import PartitionSpec as P


NT = (((1,), (1,)), ((), ()))


def product(left, right):
    return lax.dot_general(left, right, NT, preferred_element_type=jnp.float32)


def gathered(train_grads, query_grads):
    terms = jnp.einsum(
        "lqk,nlk->qn",
        lax.all_gather(query_grads, "rows", axis=1, tiled=True),
        train_grads,
        preferred_element_type=jnp.float32,
    )
    return lax.psum_scatter(terms, "layers", scatter_dimension=0, tiled=True)


def place(sizes, half, group, plan, row_ref, *refs):
    out_ref, both_ref, sem = refs[-3:]
    row = row_ref[0]
    z, x = row // 2, row % 2
    for across, low, rows, terms in plan:
        value = None
        for array, first in terms:
            term = refs[array][first : first + rows, :]
            value = term if value is None else value + term
        at = pl.multiple_of((1 - x if across else x) * sizes + low, math.gcd(sizes, low))
        both_ref[pl.ds(at, rows), :] = value
    at = pl.multiple_of(lax.rem(z + group, half) * 2 * sizes, 2 * sizes)
    copy = pltpu.make_async_copy(both_ref, out_ref.at[pl.ds(at, 2 * sizes), :], sem)
    copy.start()
    copy.wait()


def part(cut, row_ref, queries_ref, held_ref, b_ref, c_ref, sems):
    half = held_ref.shape[1]
    x = row_ref[0] % 2
    mine, other = (pl.ds(pl.multiple_of(side * half, half), half) for side in (x, 1 - x))
    copies = [
        pltpu.make_async_copy(queries_ref.at[:, mine], held_ref, sems.at[0]),
        pltpu.make_async_copy(queries_ref.at[:cut, other], b_ref, sems.at[1]),
        pltpu.make_async_copy(queries_ref.at[cut:, other], c_ref, sems.at[2]),
    ]
    for copy in copies:
        copy.start()
    for copy in copies:
        copy.wait()


def parted(row, queries, cut):
    size, depth = queries.shape
    shapes = [(size, depth // 2), (cut, depth // 2), (size - cut, depth // 2)]
    return pl.pallas_call(
        functools.partial(part, cut),
        out_shape=[pltpu.VMEM(shape, queries.dtype) for shape in shapes],
        in_specs=[pl.BlockSpec(memory_space=pltpu.SMEM), pl.BlockSpec(memory_space=pltpu.HBM)],
        out_specs=[pl.BlockSpec(memory_space=pltpu.VMEM)] * 3,
        scratch_shapes=[pltpu.SemaphoreType.DMA((3,))],
        compiler_params=pltpu.CompilerParams(vmem_limit_bytes=8 * 2**20),
        name="part",
    )(row.astype(jnp.int32).reshape(1), queries)


def paired(train_grads, query_grads):
    rows, layers = lax.axis_size("rows"), lax.axis_size("layers")
    count = rows // 2
    half = count // layers
    train = train_grads.reshape(train_grads.shape[0], -1)
    queries = jnp.swapaxes(query_grads, 0, 1).reshape(query_grads.shape[1], -1)
    size, depth = queries.shape
    row, core = lax.axis_index("rows"), lax.axis_index("layers")
    z, x = row // 2, row % 2
    ring = [(2 * ((a + 1) % count) + b, 2 * a + b) for a in range(count) for b in range(2)]
    swap = [(a, a ^ 1) for a in range(rows)]

    def move(value, hops):
        return lax.ppermute(value, "rows", hops)

    def cores(value):
        return lax.ppermute(value, "layers", [(0, 1), (1, 0)])

    def columns(value, which):
        return lax.dynamic_slice_in_dim(value, which * (depth // 2), depth // 2, 1)

    cut = size * 9 // 16
    rest = size - cut
    held, given_b, given_c = parted(row, queries, cut)
    firsts = {"A": held, "B": move(given_b, swap), "C": move(given_c, swap)}
    sides = {"O": columns(train, x), "N": move(columns(train, 1 - x), swap)}
    heights = {"A": size, "B": cut, "C": rest}
    starts = {"A": 0, "B": size, "C": size + cut}
    held_at = [firsts]
    for _ in range(1, count):
        held_at.append({piece: move(value, ring) for piece, value in held_at[-1].items()})

    def score(value, side):
        return lax.optimization_barrier(product(value, sides[side]))

    partial = {}
    for step, values in enumerate(held_at):
        for side in sides:
            if step < half:
                whole = score(jnp.concatenate(list(values.values())), side)
                for piece in values:
                    first = starts[piece]
                    partial[side, piece, step] = whole[first : first + heights[piece]]
            else:
                for piece, value in values.items():
                    partial[side, piece, step] = score(value, side)

    total = None
    for group in range(half):
        mine = lax.rem(z + group, count) // half == core
        sums, crossed = {}, {}
        for pieces in ("A", "BC") if group < half - 1 else "ABC":
            for side in "NO":
                one, two = [
                    jnp.concatenate([partial[side, piece, step] for piece in pieces]) for step in (group, group + half)
                ]
                keep, give = jnp.where(mine, one, two), jnp.where(mine, two, one)
                sums[side] = [keep, cores(give)]
            got = move(sum(sums["N"]), swap)
            first = 0
            for piece in pieces:
                for low in (0, cut) if piece == "A" else (0,):
                    crossed[piece, low] = (got, first + low)
                    sums[piece, low] = [(value, first + low) for value in sums["O"]]
                first += heights[piece]
        plan = []
        operands = []

        def index_of(value):
            for i, other in enumerate(operands):
                if other is value:
                    return i
            operands.append(value)
            return len(operands) - 1

        for mine_key, their_key, across, at, span in (
            (("A", 0), ("B", 0), False, 0, cut),
            (("A", cut), ("C", 0), False, cut, rest),
            (("B", 0), ("A", 0), True, 0, cut),
            (("C", 0), ("A", cut), True, cut, rest),
        ):
            terms = [*sums[mine_key], crossed[their_key]]
            plan.append((across, at, span, [(index_of(value), first) for value, first in terms]))
        specs = [pl.BlockSpec(memory_space=pltpu.SMEM)] + [pl.BlockSpec(memory_space=pltpu.VMEM)] * len(operands)
        aliases = {}
        if total is not None:
            aliases = {len(operands) + 1: 0}
            operands.append(total)
            specs.append(pl.BlockSpec(memory_space=pl.ANY))
        total = pl.pallas_call(
            functools.partial(place, size, half, group, plan),
            out_shape=jax.ShapeDtypeStruct((rows * size // layers, train.shape[0]), jnp.float32),
            in_specs=specs,
            out_specs=pl.BlockSpec(memory_space=pl.ANY),
            scratch_shapes=[pltpu.VMEM((2 * size, train.shape[0]), jnp.float32), pltpu.SemaphoreType.DMA],
            input_output_aliases=aliases,
            compiler_params=pltpu.CompilerParams(vmem_limit_bytes=8 * 2**20),
        )(row.astype(jnp.int32).reshape(1), *operands)
    return total


def solution(mesh):
    in_specs = (P(("groups", "rows"), "layers", None), P("layers", ("groups", "rows"), None))
    out_specs = P("layers", ("groups", "rows"))
    special = mesh.shape["rows"] == 8 and mesh.shape["layers"] == 2
    shards = paired if special else gathered
    return jax.shard_map(shards, mesh=mesh, in_specs=in_specs, out_specs=out_specs, check_vma=False)
```

```python
import functools
import math

import jax
import jax.numpy as jnp
from jax import lax
from jax.experimental import pallas as pl
from jax.experimental.pallas import tpu as pltpu
from jax.sharding import PartitionSpec as P


NT = (((1,), (1,)), ((), ()))


def product(left, right):
    return lax.dot_general(left, right, NT, preferred_element_type=jnp.float32)


def gathered(train_grads, query_grads):
    terms = jnp.einsum(
        "lqk,nlk->qn",
        lax.all_gather(query_grads, "rows", axis=1, tiled=True),
        train_grads,
        preferred_element_type=jnp.float32,
    )
    return lax.psum_scatter(terms, "layers", scatter_dimension=0, tiled=True)


def place(sizes, half, group, plan, row_ref, *refs):
    out_ref, both_ref, sem = refs[-3:]
    row = row_ref[0]
    z, x = row // 2, row % 2
    for across, low, rows, terms in plan:
        value = None
        for array, first in terms:
            term = refs[array][first : first + rows, :]
            value = term if value is None else value + term
        at = pl.multiple_of((1 - x if across else x) * sizes + low, math.gcd(sizes, low))
        both_ref[pl.ds(at, rows), :] = value
    at = pl.multiple_of(lax.rem(z + group, half) * 2 * sizes, 2 * sizes)
    copy = pltpu.make_async_copy(both_ref, out_ref.at[pl.ds(at, 2 * sizes), :], sem)
    copy.start()
    copy.wait()


def part(spans, row_ref, whole_ref, *refs):
    held_ref, given_refs, sems = refs[0], refs[1:-1], refs[-1]
    half = held_ref.shape[1]
    x = row_ref[0] % 2
    mine, other = (pl.ds(pl.multiple_of(side * half, half), half) for side in (x, 1 - x))
    copies = [pltpu.make_async_copy(whole_ref.at[:, mine], held_ref, sems.at[0])]
    for i, (first, end) in enumerate(spans):
        copies.append(pltpu.make_async_copy(whole_ref.at[first:end, other], given_refs[i], sems.at[i + 1]))
    for copy in copies:
        copy.start()
    for copy in copies:
        copy.wait()


def parted(row, whole, cuts):
    size, depth = whole.shape
    spans = list(zip((0, *cuts), (*cuts, size)))
    shapes = [(size, depth // 2)] + [(end - first, depth // 2) for first, end in spans]
    return pl.pallas_call(
        functools.partial(part, spans),
        out_shape=[pltpu.VMEM(shape, whole.dtype) for shape in shapes],
        in_specs=[pl.BlockSpec(memory_space=pltpu.SMEM), pl.BlockSpec(memory_space=pltpu.HBM)],
        out_specs=[pl.BlockSpec(memory_space=pltpu.VMEM)] * len(shapes),
        scratch_shapes=[pltpu.SemaphoreType.DMA((len(shapes),))],
        compiler_params=pltpu.CompilerParams(vmem_limit_bytes=8 * 2**20),
    )(row.astype(jnp.int32).reshape(1), pltpu.with_memory_space_constraint(whole, pltpu.HBM))


def paired(train_grads, query_grads):
    rows, layers = lax.axis_size("rows"), lax.axis_size("layers")
    count = rows // 2
    half = count // layers
    train = train_grads.reshape(train_grads.shape[0], -1)
    queries = jnp.swapaxes(query_grads, 0, 1).reshape(query_grads.shape[1], -1)
    size, _ = queries.shape
    row, core = lax.axis_index("rows"), lax.axis_index("layers")
    z = row // 2
    ring = [(2 * ((a + 1) % count) + b, 2 * a + b) for a in range(count) for b in range(2)]
    swap = [(a, a ^ 1) for a in range(rows)]

    def move(value, hops):
        return lax.ppermute(value, "rows", hops)

    def cores(value):
        return lax.ppermute(value, "layers", [(0, 1), (1, 0)])

    cut = size * 9 // 16
    rest = size - cut
    held, given_b, given_c = parted(row, queries, (cut,))
    firsts = {"A": held, "B": move(given_b, swap), "C": move(given_c, swap)}
    train_held, train_given = parted(row, train, ())
    sides = {"O": train_held, "N": move(train_given, swap)}
    heights = {"A": size, "B": cut, "C": rest}
    starts = {"A": 0, "B": size, "C": size + cut}
    held_at = [firsts]
    for _ in range(1, count):
        held_at.append({piece: move(value, ring) for piece, value in held_at[-1].items()})

    def score(value, side):
        return lax.optimization_barrier(product(value, sides[side]))

    partial = {}
    for step, values in enumerate(held_at):
        for side in sides:
            if step < half:
                whole = score(jnp.concatenate(list(values.values())), side)
                for piece in values:
                    first = starts[piece]
                    partial[side, piece, step] = whole[first : first + heights[piece]]
            else:
                for piece, value in values.items():
                    partial[side, piece, step] = score(value, side)

    total = None
    for group in range(half):
        mine = lax.rem(z + group, count) // half == core
        sums, crossed = {}, {}
        for pieces in ("A", "BC") if group < half - 1 else "ABC":
            for side in "NO":
                one, two = [
                    jnp.concatenate([partial[side, piece, step] for piece in pieces]) for step in (group, group + half)
                ]
                keep, give = jnp.where(mine, one, two), jnp.where(mine, two, one)
                sums[side] = [keep, cores(give)]
            got = move(sum(sums["N"]), swap)
            first = 0
            for piece in pieces:
                for low in (0, cut) if piece == "A" else (0,):
                    crossed[piece, low] = (got, first + low)
                    sums[piece, low] = [(value, first + low) for value in sums["O"]]
                first += heights[piece]
        plan = []
        operands = []

        def index_of(value):
            for i, other in enumerate(operands):
                if other is value:
                    return i
            operands.append(value)
            return len(operands) - 1

        for mine_key, their_key, across, at, span in (
            (("A", 0), ("B", 0), False, 0, cut),
            (("A", cut), ("C", 0), False, cut, rest),
            (("B", 0), ("A", 0), True, 0, cut),
            (("C", 0), ("A", cut), True, cut, rest),
        ):
            terms = [*sums[mine_key], crossed[their_key]]
            plan.append((across, at, span, [(index_of(value), first) for value, first in terms]))
        specs = [pl.BlockSpec(memory_space=pltpu.SMEM)] + [pl.BlockSpec(memory_space=pltpu.VMEM)] * len(operands)
        aliases = {}
        if total is not None:
            aliases = {len(operands) + 1: 0}
            operands.append(total)
            specs.append(pl.BlockSpec(memory_space=pl.ANY))
        total = pl.pallas_call(
            functools.partial(place, size, half, group, plan),
            out_shape=jax.ShapeDtypeStruct((rows * size // layers, train.shape[0]), jnp.float32),
            in_specs=specs,
            out_specs=pl.BlockSpec(memory_space=pl.ANY),
            scratch_shapes=[pltpu.VMEM((2 * size, train.shape[0]), jnp.float32), pltpu.SemaphoreType.DMA],
            input_output_aliases=aliases,
            compiler_params=pltpu.CompilerParams(vmem_limit_bytes=8 * 2**20),
        )(row.astype(jnp.int32).reshape(1), *operands)
    return total


def solution(mesh):
    in_specs = (P(("groups", "rows"), "layers", None), P("layers", ("groups", "rows"), None))
    out_specs = P("layers", ("groups", "rows"))
    special = mesh.shape["rows"] == 8 and mesh.shape["layers"] == 2
    shards = paired if special else gathered
    return jax.shard_map(shards, mesh=mesh, in_specs=in_specs, out_specs=out_specs, check_vma=False)
```

```python
import functools
import math

import jax
import jax.numpy as jnp
from jax import lax
from jax.experimental import pallas as pl
from jax.experimental.pallas import tpu as pltpu
from jax.sharding import PartitionSpec as P


NT = (((1,), (1,)), ((), ()))


def product(left, right):
    return lax.dot_general(left, right, NT, preferred_element_type=jnp.float32)


def gathered(train_grads, query_grads):
    terms = jnp.einsum(
        "lqk,nlk->qn",
        lax.all_gather(query_grads, "rows", axis=1, tiled=True),
        train_grads,
        preferred_element_type=jnp.float32,
    )
    return lax.psum_scatter(terms, "layers", scatter_dimension=0, tiled=True)


def place(sizes, half, group, plan, row_ref, *refs):
    out_ref, both_ref, sem = refs[-3:]
    row = row_ref[0]
    z, x = row // 2, row % 2
    for across, low, rows, terms in plan:
        value = None
        for array, first in terms:
            term = refs[array][first : first + rows, :]
            value = term if value is None else value + term
        at = pl.multiple_of((1 - x if across else x) * sizes + low, math.gcd(sizes, low))
        both_ref[pl.ds(at, rows), :] = value
    at = pl.multiple_of(lax.rem(z + group, half) * 2 * sizes, 2 * sizes)
    copy = pltpu.make_async_copy(both_ref, out_ref.at[pl.ds(at, 2 * sizes), :], sem)
    copy.start()
    copy.wait()


def part(spans, row_ref, whole_ref, *refs):
    held_ref, given_refs, sems = refs[0], refs[1:-1], refs[-1]
    half = held_ref.shape[1]
    x = row_ref[0] % 2
    mine, other = (pl.ds(pl.multiple_of(side * half, half), half) for side in (x, 1 - x))
    copies = [pltpu.make_async_copy(whole_ref.at[:, mine], held_ref, sems.at[0])]
    for i, (first, end) in enumerate(spans):
        copies.append(pltpu.make_async_copy(whole_ref.at[first:end, other], given_refs[i], sems.at[i + 1]))
    for copy in copies:
        copy.start()
    for copy in copies:
        copy.wait()


def parted(row, whole, cuts):
    size, depth = whole.shape
    spans = list(zip((0, *cuts), (*cuts, size)))
    shapes = [(size, depth // 2)] + [(end - first, depth // 2) for first, end in spans]
    return pl.pallas_call(
        functools.partial(part, spans),
        out_shape=[pltpu.VMEM(shape, whole.dtype) for shape in shapes],
        in_specs=[pl.BlockSpec(memory_space=pltpu.SMEM), pl.BlockSpec(memory_space=pltpu.HBM)],
        out_specs=[pl.BlockSpec(memory_space=pltpu.VMEM)] * len(shapes),
        scratch_shapes=[pltpu.SemaphoreType.DMA((len(shapes),))],
        compiler_params=pltpu.CompilerParams(vmem_limit_bytes=8 * 2**20),
    )(row.astype(jnp.int32).reshape(1), pltpu.with_memory_space_constraint(whole, pltpu.HBM))


def paired(train_grads, query_grads):
    rows, layers = lax.axis_size("rows"), lax.axis_size("layers")
    count = rows // 2
    half = count // layers
    train = train_grads.reshape(train_grads.shape[0], -1)
    queries = jnp.swapaxes(query_grads, 0, 1).reshape(query_grads.shape[1], -1)
    size, _ = queries.shape
    row, core = lax.axis_index("rows"), lax.axis_index("layers")
    z = row // 2
    ring = [(2 * ((a + 1) % count) + b, 2 * a + b) for a in range(count) for b in range(2)]
    swap = [(a, a ^ 1) for a in range(rows)]

    def move(value, hops):
        return lax.ppermute(value, "rows", hops)

    def cores(value):
        return lax.ppermute(value, "layers", [(0, 1), (1, 0)])

    cut = size * 5 // 8
    rest = size - cut
    held, given_b, given_c = parted(row, queries, (cut,))
    firsts = {"A": held, "B": move(given_b, swap), "C": move(given_c, swap)}
    train_held, train_given = parted(row, train, ())
    sides = {"O": train_held, "N": move(train_given, swap)}
    heights = {"A": size, "B": cut, "C": rest}
    starts = {"A": 0, "B": size, "C": size + cut}
    held_at = [firsts]
    back = [(target, source) for source, target in ring]
    for step in range(1, count):
        hops, values = (ring, held_at[-1]) if step < count - 1 else (back, firsts)
        held_at.append({piece: move(value, hops) for piece, value in values.items()})

    def score(value, side):
        return lax.optimization_barrier(product(value, sides[side]))

    partial = {}
    for step, values in enumerate(held_at):
        for side in sides:
            if step != half:
                whole = score(jnp.concatenate(list(values.values())), side)
                for piece in values:
                    first = starts[piece]
                    partial[side, piece, step] = whole[first : first + heights[piece]]
            else:
                for piece, value in values.items():
                    partial[side, piece, step] = score(value, side)

    total = None
    for group in reversed(range(half)):
        mine = lax.rem(z + group, count) // half == core
        sums, crossed = {}, {}
        for pieces in ("A", "BC") if group else "ABC":
            for side in "NO":
                one, two = [
                    jnp.concatenate([partial[side, piece, step] for piece in pieces]) for step in (group, group + half)
                ]
                keep, give = jnp.where(mine, one, two), jnp.where(mine, two, one)
                sums[side] = [keep, cores(give)]
            got = move(sum(sums["N"]), swap)
            first = 0
            for piece in pieces:
                for low in (0, cut) if piece == "A" else (0,):
                    crossed[piece, low] = (got, first + low)
                    sums[piece, low] = [(value, first + low) for value in sums["O"]]
                first += heights[piece]
        plan = []
        operands = []

        def index_of(value):
            for i, other in enumerate(operands):
                if other is value:
                    return i
            operands.append(value)
            return len(operands) - 1

        for mine_key, their_key, across, at, span in (
            (("A", 0), ("B", 0), False, 0, cut),
            (("A", cut), ("C", 0), False, cut, rest),
            (("B", 0), ("A", 0), True, 0, cut),
            (("C", 0), ("A", cut), True, cut, rest),
        ):
            terms = [*sums[mine_key], crossed[their_key]]
            plan.append((across, at, span, [(index_of(value), first) for value, first in terms]))
        specs = [pl.BlockSpec(memory_space=pltpu.SMEM)] + [pl.BlockSpec(memory_space=pltpu.VMEM)] * len(operands)
        aliases = {}
        if total is not None:
            aliases = {len(operands) + 1: 0}
            operands.append(total)
            specs.append(pl.BlockSpec(memory_space=pl.ANY))
        total = pl.pallas_call(
            functools.partial(place, size, half, group, plan),
            out_shape=jax.ShapeDtypeStruct((rows * size // layers, train.shape[0]), jnp.float32),
            in_specs=specs,
            out_specs=pl.BlockSpec(memory_space=pl.ANY),
            scratch_shapes=[pltpu.VMEM((2 * size, train.shape[0]), jnp.float32), pltpu.SemaphoreType.DMA],
            input_output_aliases=aliases,
            compiler_params=pltpu.CompilerParams(vmem_limit_bytes=8 * 2**20),
        )(row.astype(jnp.int32).reshape(1), *operands)
    return total


def solution(mesh):
    in_specs = (P(("groups", "rows"), "layers", None), P("layers", ("groups", "rows"), None))
    out_specs = P("layers", ("groups", "rows"))
    special = mesh.shape["rows"] == 8 and mesh.shape["layers"] == 2
    shards = paired if special else gathered
    return jax.shard_map(shards, mesh=mesh, in_specs=in_specs, out_specs=out_specs, check_vma=False)
```
